128 devices in a mesh: ctx: 16 (over z, x), tp: 8 (over y, core).
Axes of the slice: x: 4, y: 4, z: 4, core: 2. Of those that a mesh axis runs over, the one named last changes fastest.
Arguments:
- q_in: bfloat16 [8192, 8192], P('ctx', 'tp'), may hold values from -60 to 60
- k_in: bfloat16 [8192, 8192], P('ctx', 'tp'), may hold values from -6 to 6
- v_in: bfloat16 [8192, 8192], P('ctx', 'tp'), may hold values from -6 to 6
- short_filter: float32 [3, 7, 8192], P(None, None, 'tp'), may hold values from -2 to 2
- residue: float32 [16, 8192], P(None, 'tp'), may hold values from -1.2 to 1.2
- decay_rate: float32 [16, 8192], P(None, 'tp'), may hold values from 0.25 to 2048
- skip_weight: float32 [8192], P('tp'), may hold values from 0.5 to 1.5
- norm_gain: float32 [8192], P('tp'), may hold values from 0.5 to 1.5
- doc_spans: int32 [4, 2], replicated, may hold values from 0 to 8192, as said below
- cotangent: bfloat16 [8192, 8192], P('ctx', 'tp'), may hold values from -6 to 6
Outputs:
- mixed_out: bfloat16 [8192, 8192], P('ctx', 'tp')
- grad_q: bfloat16 [8192, 8192], P('ctx', 'tp')
- grad_k: bfloat16 [8192, 8192], P('ctx', 'tp')
- grad_v: bfloat16 [8192, 8192], P('ctx', 'tp')
The draws below stay inside these ranges and needn't reach their ends.
Inputs may be any that keep to these rules, and one draw needn't show every extreme that they name: `doc_spans`: row d holds the first position and the end (exclusive) of document d; the documents follow one another in order without gaps, the first starts at 0, the last ends at 8192, and none is empty.
All inputs are finite; a program needn't handle non-finite values.
Results may differ from the reference program's by a relative error of at most 0.001.
Values may be sent and summed in bfloat16 or wider, within the bound.
A program may use at most 64 MiB of HBM per device.

```python
import jax
import jax.numpy as jnp
from jax import lax

D = 8192
KS = 7
R = 16
NDOC = 4
SEQ = 8192
N_TP = 8


def draw_q_in(key, part):
    key_noise, key_rows = jax.random.split(key, 2)
    columns = jnp.arange(D, dtype=jnp.float32) / D - 0.5
    row_draw = jax.random.uniform(key_rows, (SEQ, 1), jnp.float32)
    base_values = jnp.clip(jax.random.normal(key_noise, (SEQ, D), jnp.float32), -6.0, 6.0)
    col_scale = jnp.exp(jnp.log(10.0) * columns)
    row_scale = jnp.exp(jnp.log(10.0) * (row_draw - 0.5))
    return (base_values * col_scale[None, :] * row_scale).astype(jnp.bfloat16)


def draw_decay_rate(key, part):
    key_jitter, key_order = jax.random.split(key, 2)
    jitter = jax.random.uniform(key_jitter, (R, D), jnp.float32)
    strata = jnp.arange(R, dtype=jnp.float32)[:, None]
    low_end = jnp.log(0.25)
    top_end = jnp.log(SEQ / 4.0)
    log_rates = low_end + (strata + jitter) / R * (top_end - low_end)
    log_rates = jnp.clip(log_rates, low_end, top_end)
    shuffled = jax.random.permutation(key_order, log_rates, axis=0, independent=True)
    return jnp.exp(shuffled).astype(jnp.float32)


def draw_doc_spans(key, part):
    picks = jax.random.permutation(key, SEQ - 1)[:NDOC - 1] + 1
    cuts = jnp.sort(picks).astype(jnp.int32)
    starts = jnp.concatenate([jnp.zeros((1,), jnp.int32), cuts])
    finishes = jnp.concatenate([cuts, jnp.full((1,), SEQ, jnp.int32)])
    return jnp.stack([starts, finishes], axis=1)


def block_levels(own_key, shape, cuts, smallest, top_value):
    loudness = 1.0
    for axis_at, shards_of in cuts:
        heights = jax.random.uniform(jax.random.fold_in(jax.random.fold_in(own_key, 6), axis_at), (shards_of,), jnp.float32, smallest / len(cuts), top_value / len(cuts))
        loudness = loudness * jnp.repeat(jnp.exp(heights), shape[axis_at] // shards_of).reshape((-1,) + (1,) * (len(shape) - 1 - axis_at))
    return loudness


def normal_values(key, extent, width, bound, pieces=(), kind=jnp.bfloat16):
    loudness = block_levels(key, extent, pieces, -0.22, 0.18) if pieces else 1.0
    values = jax.random.normal(key, extent, jnp.float32) * width * loudness
    return jnp.minimum(jnp.maximum(values, -bound), bound).astype(kind)


def setup_inputs(seed: int = 0) -> dict:
    arg_keys = jax.random.split(jax.random.key(seed), 11)
    q_in = draw_q_in(jax.random.fold_in(arg_keys[10], 71), 0)
    k_in = normal_values(arg_keys[1], (SEQ, D), 1.0, 6.0, ((0, 16), (1, 8)))
    v_in = normal_values(arg_keys[2], (SEQ, D), 1.0, 6.0, ((0, 16), (1, 8)))
    short_filter = normal_values(arg_keys[3], (3, KS, D), KS ** -0.5, 2.0, ((2, 8),), jnp.float32)
    residue = jnp.clip(jax.random.uniform(arg_keys[4], (R, D), jnp.float32, -1.2, 1.2) * block_levels(arg_keys[4], (R, D), ((1, 8),), -0.4, 0.0), -1.2, 1.2)
    decay_rate = draw_decay_rate(jax.random.fold_in(arg_keys[10], 71), 0)
    skip_weight = jnp.clip(0.5 + 1.0 * jax.random.uniform(arg_keys[6], (D,), jnp.float32) ** block_levels(arg_keys[6], (D,), ((0, 8),), -0.2, 0.2), 0.5, 1.5)
    norm_gain = jnp.clip(1.0 + 0.1 * jax.random.normal(arg_keys[7], (D,), jnp.float32), 0.5, 1.5)
    doc_spans = draw_doc_spans(jax.random.fold_in(arg_keys[10], 71), 0)
    cotangent = normal_values(arg_keys[9], (SEQ, D), 1.0, 6.0, ((0, 16), (1, 8)))
    return dict(q_in=q_in, k_in=k_in, v_in=v_in, short_filter=short_filter, residue=residue, decay_rate=decay_rate, skip_weight=skip_weight, norm_gain=norm_gain, doc_spans=doc_spans, cotangent=cotangent)


def doc_bounds(doc_spans, positions, seq_total):
    starts = doc_spans[:, 0]
    finishes = doc_spans[:, 1]
    begins = lax.optimization_barrier(jnp.max(jnp.where(starts[:, None] <= positions[None, :], starts[:, None], 0), axis=0))
    ends_at = lax.optimization_barrier(jnp.min(jnp.where(finishes[:, None] > positions[None, :], finishes[:, None], seq_total), axis=0))
    return (begins.astype(jnp.int32), ends_at.astype(jnp.int32))

def featurize(stream, kernel, positions, begins):
    length = stream.shape[0]
    result = jnp.zeros(stream.shape, jnp.float32)
    for tap_index in range(KS):
        shifted = jnp.concatenate([jnp.zeros((tap_index, stream.shape[1]), jnp.float32), stream[:length - tap_index].astype(jnp.float32)], axis=0)
        valid_rows = (positions - tap_index >= begins)[:, None]
        result = result + kernel[tap_index][None, :] * jnp.where(valid_rows, shifted, 0.0)
    return result

def transpose_featurize(grad_rows, kernel, positions, begins):
    length = grad_rows.shape[0]
    result = jnp.zeros(grad_rows.shape, jnp.float32)
    for tap_index in range(KS):
        shifted = jnp.concatenate([grad_rows[tap_index:], jnp.zeros((tap_index, grad_rows.shape[1]), jnp.float32)], axis=0)
        later_begin = jnp.concatenate([begins[tap_index:], jnp.full((tap_index,), length, jnp.int32)], axis=0)
        valid_rows = (later_begin <= positions)[:, None]
        result = result + kernel[tap_index][None, :] * jnp.where(valid_rows, shifted, 0.0)
    return result

def modal_sweep(source, restart, decays, amplitudes, backward):
    factors = jnp.exp(-decays)

    def scan_step(carry_state, step_inputs):
        value_row, fresh = step_inputs
        carry_state = jnp.where(fresh, 0.0, factors * carry_state) + value_row[None, :]
        return (carry_state, lax.optimization_barrier(jnp.sum(amplitudes * carry_state, axis=0)))
    _, swept = lax.scan(scan_step, jnp.zeros(decays.shape, jnp.float32), (source, restart), reverse=backward)
    return swept

def reference(q_in, k_in, v_in, short_filter, residue, decay_rate, skip_weight, norm_gain, doc_spans, cotangent):
    positions = jnp.arange(SEQ, dtype=jnp.int32)
    begins, ends_at = doc_bounds(doc_spans, positions, SEQ)
    first_rows = begins == positions
    last_rows = ends_at == positions + 1
    decays = decay_rate / SEQ
    amplitudes = residue * jnp.sqrt(decay_rate / SEQ)
    groups = N_TP
    group_width = D // groups

    def split_columns(array):
        return jnp.moveaxis(array.reshape(array.shape[:-1] + (groups, group_width)), -2, 0)

    def join_columns(parts):
        return jnp.moveaxis(parts, 0, -2).reshape(SEQ, D)
    shared = (split_columns(q_in), split_columns(k_in), split_columns(v_in), split_columns(short_filter), split_columns(decays), split_columns(amplitudes), split_columns(skip_weight))
    gain_parts = split_columns(norm_gain)
    cot_parts = split_columns(cotangent)

    def forward_group(group_inputs):
        q_part, k_part, v_part, taps, decay_part, amp_part, skip_part = group_inputs
        feat_q = featurize(q_part, taps[0], positions, begins)
        feat_k = featurize(k_part, taps[1], positions, begins)
        feat_v = featurize(v_part, taps[2], positions, begins)
        inner_term = feat_k * feat_v
        long_term = modal_sweep(inner_term, first_rows, decay_part, amp_part, False)
        mix_term = long_term + skip_part[None, :] * inner_term
        return (feat_q, feat_k, feat_v, mix_term)

    def gated_group(group_inputs):
        feat_q, feat_k, feat_v, mix_term = forward_group(group_inputs)
        return feat_q * mix_term
    gated_parts = lax.map(gated_group, shared)
    inv_rms = lax.rsqrt(lax.optimization_barrier(jnp.sum(gated_parts * gated_parts, axis=(0, 2))) / D + 1e-06)
    mixed_out = join_columns(gated_parts * inv_rms[None, :, None] * gain_parts[:, None, :]).astype(jnp.bfloat16)
    weighted = cot_parts.astype(jnp.float32) * gain_parts[:, None, :]
    cross_mean = lax.optimization_barrier(jnp.sum(weighted * gated_parts, axis=(0, 2))) / D
    grad_gated = inv_rms[None, :, None] * weighted - gated_parts * (inv_rms ** 3 * cross_mean)[None, :, None]

    def backward_group(both_inputs):
        group_inputs, grad_part = both_inputs
        feat_q, feat_k, feat_v, mix_term = forward_group(group_inputs)
        taps, decay_part, amp_part, skip_part = group_inputs[3:]
        grad_qf = grad_part * mix_term
        grad_mix = grad_part * feat_q
        grad_inner = skip_part[None, :] * grad_mix + modal_sweep(grad_mix, last_rows, decay_part, amp_part, True)
        grad_kf = grad_inner * feat_v
        grad_vf = grad_inner * feat_k
        return (transpose_featurize(grad_qf, taps[0], positions, begins).astype(jnp.bfloat16), transpose_featurize(grad_kf, taps[1], positions, begins).astype(jnp.bfloat16), transpose_featurize(grad_vf, taps[2], positions, begins).astype(jnp.bfloat16))
    grad_parts = lax.map(backward_group, (shared, grad_gated))
    return (mixed_out, join_columns(grad_parts[0]), join_columns(grad_parts[1]), join_columns(grad_parts[2]))
```

```python
import functools

import jax
import jax.numpy as jnp
from jax import lax
from jax.experimental import pallas as pl
from jax.experimental.pallas import tpu as pltpu
from jax.sharding import PartitionSpec as P

MESH = pl.DeviceIdType.MESH
F32 = jnp.float32
LANES = 128
SUB = 8


def tree_sum(terms):
    while len(terms) > 1:
        paired = [terms[i] + terms[i + 1] for i in range(0, len(terms) - 1, 2)]
        if len(terms) % 2:
            paired.append(terms[-1])
        terms = paired
    return terms[0]


def row(ref, t):
    return ref[pl.ds(pl.multiple_of(t * SUB, SUB), SUB), :]


def put_row(ref, t, value):
    ref[pl.ds(pl.multiple_of(t * SUB, SUB), SUB), :] = value


def turned(ref, block, s):
    return ref[pl.ds(block * SUB * SUB + s, SUB, stride=SUB), :]


def scalar_first(spans, docs, t):
    first = jnp.int32(0)
    for d in range(1, docs):
        start = spans[d, 0]
        first = jnp.where(start <= t, jnp.maximum(first, start), first)
    return first


def scalar_end(spans, docs, t, total):
    end = jnp.int32(total)
    for d in range(docs - 1):
        finish = spans[d, 1]
        end = jnp.where(finish > t, jnp.minimum(end, finish), end)
    return end


def kernel(
    sizes,
    q_hbm,
    k_hbm,
    v_hbm,
    c_hbm,
    taps_ref,
    residue_ref,
    decay_ref,
    skip_ref,
    gain_ref,
    spans,
    mixed_hbm,
    gq_hbm,
    gk_hbm,
    gv_hbm,
    qb,
    kb,
    vb,
    cb,
    halo,
    flq,
    flk,
    flv,
    flc,
    fq,
    fk,
    fv,
    inner,
    mix,
    gated,
    gmix,
    gradq,
    gradk,
    gradv,
    back,
    ob,
    wt,
    ft,
    par,
    ptmp,
    gaint,
    alpha,
    beta,
    sums_tx,
    sums_rx,
    s1tx,
    s1rx,
    s2tx,
    s2rx,
    vidx,
    sidx,
    in_sem,
    out_sem,
    idx_sem,
    halo_send,
    halo_recv,
    state_send,
    state_recv,
    sum_send,
    sum_recv,
    grad_send,
    grad_recv,
):
    n_ctx, n_tp, rows, docs, modes, reach = sizes
    blocks = rows // SUB
    groups = SUB
    total_rows = rows * n_ctx
    width = groups * LANES * n_tp
    me = lax.axis_index("ctx")
    me_tp = lax.axis_index("tp")
    first_row = me * rows
    last_row = first_row + rows - 1
    after = lax.rem(me + 1, n_ctx)
    before = lax.rem(me + n_ctx - 1, n_ctx)

    barrier = pltpu.get_barrier_semaphore()
    for d in range(1, n_ctx):
        pl.semaphore_signal(
            barrier, inc=1, device_id={"ctx": lax.rem(me + d, n_ctx)}, device_id_type=MESH
        )
    for d in range(1, n_tp):
        pl.semaphore_signal(
            barrier, inc=1, device_id={"tp": lax.rem(me_tp + d, n_tp)}, device_id_type=MESH
        )

    loads = [
        pltpu.make_async_copy(src, dst, in_sem.at[i])
        for i, (src, dst) in enumerate(((k_hbm, kb), (v_hbm, vb), (q_hbm, qb), (c_hbm, cb)))
    ]
    for copy in loads:
        copy.start()

    at = first_row + (
        lax.broadcasted_iota(jnp.int32, (SUB, LANES), 0) * LANES
        + lax.broadcasted_iota(jnp.int32, (SUB, LANES), 1)
    )
    begin_v = jnp.zeros((SUB, LANES), jnp.int32)
    for d in range(1, docs):
        start = spans[d, 0]
        begin_v = jnp.where(start <= at, jnp.maximum(begin_v, start), begin_v)
    end_v = jnp.full((SUB, LANES), total_rows, jnp.int32)
    for d in range(docs - 1):
        finish = spans[d, 1]
        end_v = jnp.where(finish > at, jnp.minimum(end_v, finish), end_v)
    vidx[0] = jnp.minimum(at - begin_v, reach)
    vidx[1] = jnp.minimum(end_v - 1 - at, reach)
    idx_copy = pltpu.make_async_copy(vidx, sidx, idx_sem)
    idx_copy.start()

    b_first = scalar_first(spans, docs, first_row)
    e_first = scalar_end(spans, docs, first_row, total_rows)
    b_last = scalar_first(spans, docs, last_row)
    e_last = scalar_end(spans, docs, last_row, total_rows)
    open_front = jnp.where(b_first < first_row, e_first - first_row, 0)
    open_back = jnp.where(e_last > last_row + 1, b_last - first_row, rows)
    tail_from = b_last - first_row
    head_to = e_first - first_row

    def spread(src, count, base):
        for g in range(groups):
            ptmp[pl.ds(g * SUB, count), :] = src[:, g * LANES : (g + 1) * LANES]
        return [ptmp[pl.ds(s, SUB, stride=SUB), :] for s in range(count)]

    DEC, AMP, FAR, JUMP = 0, modes, 2 * modes, 3 * modes
    for half in range(modes // SUB):
        cols = spread(decay_ref.at[pl.ds(half * SUB, SUB), :], SUB, 0)
        ress = spread(residue_ref.at[pl.ds(half * SUB, SUB), :], SUB, 0)
        for s in range(SUB):
            r = half * SUB + s
            decay = cols[s] / total_rows
            par[AMP + r] = ress[s] * jnp.sqrt(decay)
            factor = jnp.exp(-decay)
            par[DEC + r] = factor
            par[FAR + r] = jnp.exp(-decay * (rows - SUB))
            par[JUMP + r] = jnp.exp(-decay * rows)
            ft[0, r] = jnp.zeros((SUB, LANES), F32)
            ft[1, r] = factor
    for stream in range(3):
        taps = spread(taps_ref.at[stream], reach + 1, 0)
        for pattern in range(reach + 1):
            for j in range(reach + 1):
                wt[pattern, stream, j] = (
                    taps[j] if j <= pattern else jnp.zeros((SUB, LANES), F32)
                )
    for g in range(groups):
        gaint[pl.ds(g * SUB, SUB), :] = jnp.broadcast_to(gain_ref[g : g + 1, :], (SUB, LANES))

    pl.semaphore_wait(barrier, n_ctx - 1 + n_tp - 1)

    halo_copies = []
    for i, src in enumerate((k_hbm, v_hbm, q_hbm)):
        copy = pltpu.make_async_remote_copy(
            src_ref=src.at[pl.ds(rows - 16, 16), :],
            dst_ref=halo.at[i],
            send_sem=halo_send.at[i],
            recv_sem=halo_recv.at[i],
            device_id={"ctx": after},
            device_id_type=MESH,
        )
        copy.start()
        halo_copies.append(copy)

    def lift(src, dst):
        def body(i, _):
            for g in range(groups):
                both = src[
                    pl.ds(pl.multiple_of(i * 16, 16), 16), g * LANES : (g + 1) * LANES
                ].astype(F32)
                for h in range(2):
                    dst[
                        pl.ds(
                            pl.multiple_of(((2 * i + 2 + h) * groups + g) * SUB, SUB), SUB
                        ),
                        :,
                    ] = both[h * SUB : (h + 1) * SUB]
            return 0

        lax.fori_loop(0, rows // 16, body, 0)

    def lift_halo(src, dst):
        for g in range(groups):
            both = src[:, g * LANES : (g + 1) * LANES].astype(F32)
            for h in range(2):
                dst[pl.ds((h * groups + g) * SUB, SUB), :] = both[h * SUB : (h + 1) * SUB]

    def index_of(which, t):
        return sidx[which, lax.div(t, LANES), lax.rem(t, LANES)]

    def fir_rows(src, stream, b, patterns):
        xs = [turned(src, b + 1, s) for s in range(SUB - reach, SUB)]
        xs += [turned(src, b + 2, s) for s in range(SUB)]
        out = []
        for s in range(SUB):
            terms = [
                wt[patterns[s], stream, j] * xs[s + reach - j] for j in range(reach + 1)
            ]
            out.append(tree_sum(terms))
        return out

    def featurize_kv(b):
        patterns = [index_of(0, b * SUB + s) for s in range(SUB)]
        ks = fir_rows(flk, 1, b, patterns)
        vs = fir_rows(flv, 2, b, patterns)
        for s in range(SUB):
            t = b * SUB + s
            put_row(fk, t, ks[s])
            put_row(fv, t, vs[s])
            put_row(inner, t, ks[s] * vs[s])

    def featurize_q(b):
        patterns = [index_of(0, b * SUB + s) for s in range(SUB)]
        qs = fir_rows(flq, 0, b, patterns)
        for s in range(SUB):
            put_row(fq, b * SUB + s, qs[s])

    def loop(lo, hi, step):
        def body(i, _):
            step(i)
            return 0

        lax.fori_loop(lo, hi, body, 0)

    loads[0].wait()
    lift(kb, flk)
    loads[1].wait()
    lift(vb, flv)
    idx_copy.wait()
    loop(1, blocks, featurize_kv)

    factors = [par[DEC + r] for r in range(modes)]
    zeros = tuple(jnp.zeros((SUB, LANES), F32) for _ in range(modes))

    def end_rows(source, states, b, forward, keep):
        states = list(states)
        order = range(SUB) if forward else range(SUB - 1, -1, -1)
        for s in order:
            t = b * SUB + s
            x = row(source, t)
            x = x * jnp.where(keep(t), jnp.float32(1.0), jnp.float32(0.0))
            states = [f * st + x for f, st in zip(factors, states)]
        return tuple(states)

    in_tail = lambda t: t >= tail_from
    ends = lax.fori_loop(
        1, blocks, lambda b, st: end_rows(inner, st, b, True, in_tail), zeros
    )
    for copy in halo_copies:
        copy.wait()
    lift_halo(halo.at[0], flk)
    lift_halo(halo.at[1], flv)
    lift_halo(halo.at[2], flq)
    featurize_kv(0)
    heads = end_rows(inner, zeros, 0, True, in_tail)
    for r in range(modes):
        s1tx[0, r] = ends[r] + par[FAR + r] * heads[r]

    def send_all(direction, phase, src, dst):
        copies = []
        for d in range(1, n_ctx):
            target = lax.rem(me + d, n_ctx)
            copy = pltpu.make_async_remote_copy(
                src_ref=src.at[direction, target],
                dst_ref=dst.at[direction, me],
                send_sem=state_send.at[direction, phase, d],
                recv_sem=state_recv.at[direction, phase, d],
                device_id={"ctx": target},
                device_id_type=MESH,
            )
            copy.start()
            copies.append(copy)
        return copies

    def fold(direction):
        jump = par[JUMP + me]
        state = jnp.zeros((SUB, LANES), F32)
        order = range(n_ctx) if direction == 0 else range(n_ctx - 1, -1, -1)
        for i in order:
            s2tx[direction, i] = state
            lo = i * rows
            if direction == 0:
                through = scalar_first(spans, docs, lo + rows - 1) < lo
            else:
                through = scalar_end(spans, docs, lo, total_rows) > lo + rows
            flag = jnp.where(through, jnp.float32(1.0), jnp.float32(0.0))
            state = (jump * flag) * state + s1rx[direction, i]

    def scan_rows(source, states, b, forward, store):
        states = list(states)
        order = range(SUB) if forward else range(SUB - 1, -1, -1)
        for s in order:
            t = b * SUB + s
            x = row(source, t)
            keep = jnp.minimum(index_of(0 if forward else 1, t), 1)
            states = [ft[keep, r] * st + x for r, st in enumerate(states)]
            y = tree_sum([a * st for a, st in zip(amps, states)])
            store(t, y + skip * x)
        return tuple(states)

    amps = [par[AMP + r] for r in range(modes)]
    skip = skip_ref[...]

    sent = send_all(0, 0, s1tx, s1rx)

    loads[2].wait()
    lift(qb, flq)
    loop(0, blocks, featurize_q)
    loads[3].wait()

    def lift_cot(i, _):
        for g in range(groups):
            both = cb[pl.ds(pl.multiple_of(i * 16, 16), 16), g * LANES : (g + 1) * LANES].astype(
                F32
            )
            for h in range(2):
                flc[
                    pl.ds(pl.multiple_of(((2 * i + h) * groups + g) * SUB, SUB), SUB), :
                ] = both[h * SUB : (h + 1) * SUB] * gaint[pl.ds(g * SUB, SUB), :]
        return 0

    lax.fori_loop(0, rows // 16, lift_cot, 0)

    for copy in sent:
        copy.wait()
    s1rx[0, me] = s1tx[0, me]
    fold(0)
    sent = send_all(0, 1, s2tx, s2rx)
    lax.fori_loop(
        0,
        blocks,
        lambda b, st: scan_rows(
            inner, st, b, True, lambda t, y: put_row(mix, t, y)
        ),
        zeros,
    )
    for copy in sent:
        copy.wait()
    s2rx[0, me] = s2tx[0, me]

    def correct(b, incs):
        incs = list(incs)
        for s in range(SUB):
            t = b * SUB + s
            incs = [f * c for f, c in zip(factors, incs)]
            flag = jnp.where(t < open_front, jnp.float32(1.0), jnp.float32(0.0))
            m = row(mix, t) + flag * tree_sum(incs)
            put_row(mix, t, m)
            put_row(gated, t, m * row(fq, t))
        return tuple(incs)

    lax.fori_loop(
        0, blocks, correct, tuple(amps[r] * s2rx[0, r] for r in range(modes))
    )

    lane = lax.broadcasted_iota(jnp.int32, (SUB, LANES), 1)

    def row_sums(b, acc):
        gs = [turned(gated, b, g) for g in range(groups)]
        ws = [row(flc, b * groups + g) for g in range(groups)]
        squares = tree_sum([g * g for g in gs])
        cross = tree_sum([g * w for g, w in zip(gs, ws)])
        acc = jnp.where(lane == b, jnp.sum(squares, axis=1, keepdims=True), acc)
        return jnp.where(lane == b + blocks, jnp.sum(cross, axis=1, keepdims=True), acc)

    sums_tx[...] = lax.fori_loop(0, blocks, row_sums, jnp.zeros((SUB, LANES), F32))
    sent = []
    for d in range(1, n_tp):
        copy = pltpu.make_async_remote_copy(
            src_ref=sums_tx,
            dst_ref=sums_rx.at[me_tp],
            send_sem=sum_send.at[d],
            recv_sem=sum_recv.at[d],
            device_id={"tp": lax.rem(me_tp + d, n_tp)},
            device_id_type=MESH,
        )
        copy.start()
        sent.append(copy)
    for copy in sent:
        copy.wait()
    sums_rx[me_tp] = sums_tx[...]
    total = tree_sum([sums_rx[i] for i in range(n_tp)])
    inv_rms = lax.rsqrt(total / width + 1e-6)
    cross = pltpu.roll(total, LANES - blocks, 1)
    cubed = inv_rms * inv_rms * inv_rms * cross / width
    for b in range(blocks):
        alpha[pl.ds(b * SUB, SUB), :] = jnp.broadcast_to(inv_rms[:, b : b + 1], (SUB, LANES))
        beta[pl.ds(b * SUB, SUB), :] = jnp.broadcast_to(cubed[:, b : b + 1], (SUB, LANES))

    in_head = lambda t: t < head_to

    def grads(i, states):
        b = blocks - 1 - i
        for s in range(SUB):
            t = b * SUB + s
            al = alpha[pl.ds(t, SUB, stride=0), :]
            be = beta[pl.ds(t, SUB, stride=0), :]
            grad = al * turned(flc, b, s) - be * row(gated, t)
            put_row(gradq, t, grad * row(mix, t))
            put_row(gmix, t, grad * row(fq, t))
        return end_rows(gmix, states, b, False, in_head)

    ends = lax.fori_loop(0, blocks, grads, zeros)
    for r in range(modes):
        s1tx[1, r] = ends[r]
    sent = send_all(1, 0, s1tx, s1rx)

    def send_halo(i, src):
        copy = pltpu.make_async_remote_copy(
            src_ref=src.at[pl.ds(0, SUB * SUB), :],
            dst_ref=src.at[pl.ds(rows * SUB, SUB * SUB), :],
            send_sem=grad_send.at[i],
            recv_sem=grad_recv.at[i],
            device_id={"ctx": before},
            device_id_type=MESH,
        )
        copy.start()
        return copy

    grad_copies = [send_halo(0, gradq)]

    def lower_mixed(i, _):
        for g in range(groups):
            halves = []
            for h in range(2):
                b = 2 * i + h
                al = alpha[pl.ds(pl.multiple_of(b * SUB, SUB), SUB), :]
                halves.append(turned(gated, b, g) * al * gaint[pl.ds(g * SUB, SUB), :])
            ob[
                0, pl.ds(pl.multiple_of(i * 16, 16), 16), g * LANES : (g + 1) * LANES
            ] = jnp.concatenate(halves, axis=0).astype(jnp.bfloat16)
        return 0

    lax.fori_loop(0, rows // 16, lower_mixed, 0)
    outs = [pltpu.make_async_copy(ob.at[0], mixed_hbm, out_sem.at[0])]
    outs[0].start()

    for copy in sent:
        copy.wait()
    s1rx[1, me] = s1tx[1, me]
    fold(1)
    sent = send_all(1, 1, s2tx, s2rx)

    lax.fori_loop(
        0,
        blocks,
        lambda i, st: scan_rows(
            gmix, st, blocks - 1 - i, False, lambda t, y: put_row(back, t, y)
        ),
        zeros,
    )

    def transposed(src, stream, dst):
        def step(b):
            patterns = [index_of(1, b * SUB + s) for s in range(SUB)]
            xs = [row(src, b * SUB + s) for s in range(SUB + reach)]
            for s in range(SUB):
                terms = [wt[patterns[s], stream, j] * xs[s + j] for j in range(reach + 1)]
                put_row(dst, b * SUB + s, tree_sum(terms))

        return step

    def lower(src, slot):
        def step(i):
            for g in range(groups):
                both = jnp.concatenate(
                    [turned(src, 2 * i, g), turned(src, 2 * i + 1, g)], axis=0
                )
                ob[
                    slot, pl.ds(pl.multiple_of(i * 16, 16), 16), g * LANES : (g + 1) * LANES
                ] = both.astype(jnp.bfloat16)

        return step

    grad_copies[0].wait()
    step_q = transposed(gradq, 0, flc)
    loop(0, blocks, step_q)
    loop(0, rows // 16, lower(flc, 1))
    outs.append(pltpu.make_async_copy(ob.at[1], gq_hbm, out_sem.at[1]))
    outs[1].start()

    for copy in sent:
        copy.wait()
    s2rx[1, me] = s2tx[1, me]

    def correct_back(b, incs):
        incs = list(incs)
        for s in range(SUB - 1, -1, -1):
            t = b * SUB + s
            incs = [f * c for f, c in zip(factors, incs)]
            flag = jnp.where(t >= open_back, jnp.float32(1.0), jnp.float32(0.0))
            grad = row(back, t) + flag * tree_sum(incs)
            put_row(gradk, t, grad * row(fv, t))
            put_row(gradv, t, grad * row(fk, t))
        return tuple(incs)

    incs = tuple(amps[r] * s2rx[1, r] for r in range(modes))
    correct_back(0, tuple(par[FAR + r] * incs[r] for r in range(modes)))
    grad_copies.append(send_halo(1, gradk))
    grad_copies.append(send_halo(2, gradv))
    lax.fori_loop(0, blocks - 1, lambda i, c: correct_back(blocks - 1 - i, c), incs)
    for i, (src, stage, dst) in enumerate(((gradk, flk, gk_hbm), (gradv, flv, gv_hbm))):
        step = transposed(src, 1 + i, stage)
        grad_copies[1 + i].wait()
        loop(0, blocks, step)
        loop(0, rows // 16, lower(stage, 2 + i))
        outs.append(pltpu.make_async_copy(ob.at[2 + i], dst, out_sem.at[2 + i]))
        outs[-1].start()
    for copy in outs:
        copy.wait()


def solution(mesh):
    n_ctx, n_tp = mesh.shape["ctx"], mesh.shape["tp"]

    def local(q, k, v, taps, residue, decay, skip, gain, spans, cot):
        rows, cols = q.shape
        modes, docs, reach = residue.shape[0], spans.shape[0], taps.shape[1] - 1
        assert cols == SUB * LANES and modes == n_ctx and rows % 16 == 0
        assert rows // SUB * 2 <= LANES and rows <= SUB * LANES and modes % SUB == 0
        flat = (rows * SUB, LANES)
        front = ((rows + 16) * SUB, LANES)
        tail = ((rows + SUB) * SUB, LANES)
        V = pltpu.VMEM
        D = pltpu.SemaphoreType.DMA
        tile = (SUB, LANES)
        scratch = (
            [V((rows, cols), jnp.bfloat16)] * 4
            + [V((3, 16, cols), jnp.bfloat16)]
            + [V(front, F32)] * 3
            + [V(flat, F32)] * 8
            + [V(tail, F32)] * 3
            + [V(flat, F32)]
            + [V((4, rows, cols), jnp.bfloat16)]
            + [
                V((reach + 1, 3, reach + 1) + tile, F32),
                V((2, modes) + tile, F32),
                V((4 * modes,) + tile, F32),
                V((SUB * SUB, LANES), F32),
                V((SUB * SUB, LANES), F32),
                V((rows + SUB, LANES), F32),
                V((rows + SUB, LANES), F32),
                V(tile, F32),
                V((n_tp,) + tile, F32),
                V((2, n_ctx) + tile, F32),
                V((2, n_ctx) + tile, F32),
                V((2, n_ctx) + tile, F32),
                V((2, n_ctx) + tile, F32),
                V((2,) + tile, jnp.int32),
                pltpu.SMEM((2,) + tile, jnp.int32),
                D((4,)),
                D((4,)),
                D,
                D((3,)),
                D((3,)),
                D((2, 2, n_ctx)),
                D((2, 2, n_ctx)),
                D((n_tp,)),
                D((n_tp,)),
                D((3,)),
                D((3,)),
            ]
        )
        hbm = pl.BlockSpec(memory_space=pl.ANY)
        vmem = pl.BlockSpec(memory_space=pltpu.VMEM)
        out = jax.ShapeDtypeStruct((rows, cols), jnp.bfloat16)
        sizes = (n_ctx, n_tp, rows, docs, modes, reach)
        return pl.pallas_call(
            functools.partial(kernel, sizes),
            out_shape=(out,) * 4,
            in_specs=[hbm] * 4 + [vmem] * 5 + [pl.BlockSpec(memory_space=pltpu.SMEM)],
            out_specs=(hbm,) * 4,
            scratch_shapes=scratch,
            compiler_params=pltpu.CompilerParams(
                collective_id=0, has_side_effects=True, vmem_limit_bytes=60 * 1024 * 1024
            ),
            name="hyena",
        )(
            q,
            k,
            v,
            cot,
            taps,
            residue,
            decay,
            skip.reshape(SUB, LANES),
            gain.reshape(SUB, LANES),
            spans,
        )

    placed = (
        P("ctx", "tp"),
        P("ctx", "tp"),
        P("ctx", "tp"),
        P(None, None, "tp"),
        P(None, "tp"),
        P(None, "tp"),
        P("tp"),
        P("tp"),
        P(),
        P("ctx", "tp"),
    )
    return jax.shard_map(
        local,
        mesh=mesh,
        in_specs=placed,
        out_specs=(P("ctx", "tp"),) * 4,
        check_vma=False,
    )
```

```python
import functools

import jax
import jax.numpy as jnp
from jax import lax
from jax.experimental import pallas as pl
from jax.experimental.pallas import tpu as pltpu
from jax.sharding import PartitionSpec as P

MESH = pl.DeviceIdType.MESH
F32 = jnp.float32
LANES = 128
SUB = 8
GRANT = 40 * 1024 * 1024
LAST_GRANT = 20 * 1024 * 1024


def tree_sum(terms):
    while len(terms) > 1:
        paired = [terms[i] + terms[i + 1] for i in range(0, len(terms) - 1, 2)]
        if len(terms) % 2:
            paired.append(terms[-1])
        terms = paired
    return terms[0]


def row(ref, t):
    return ref[pl.ds(pl.multiple_of(t * SUB, SUB), SUB), :]


def put_row(ref, t, value):
    ref[pl.ds(pl.multiple_of(t * SUB, SUB), SUB), :] = value


def turned(ref, block, s):
    return ref[pl.ds(block * SUB * SUB + s, SUB, stride=SUB), :]


def scalar_first(spans, docs, t):
    first = jnp.int32(0)
    for d in range(1, docs):
        start = spans[0, d]
        first = jnp.where(start <= t, jnp.maximum(first, start), first)
    return first


def scalar_end(spans, docs, t, total):
    end = jnp.int32(total)
    for d in range(docs - 1):
        finish = spans[1, d]
        end = jnp.where(finish > t, jnp.minimum(end, finish), end)
    return end


def kernel(
    sizes,
    q_hbm,
    k_hbm,
    v_hbm,
    c_hbm,
    taps_hbm,
    residue_hbm,
    decay_hbm,
    skip_hbm,
    gain_hbm,
    spans_hbm,
    gradq,
    gradk,
    gradv,
    gated,
    alpha,
    qb,
    kb,
    vb,
    cb,
    halo,
    flq,
    flk,
    flv,
    flc,
    fq,
    fk,
    fv,
    inner,
    mix,
    gmix,
    back,
    ghalo,
    wt,
    ft,
    par,
    ptmp,
    gaint,
    beta,
    in_tail,
    in_head,
    in_front,
    in_back,
    sums_tx,
    sums_rx,
    s1tx,
    s1rx,
    s2tx,
    s2rx,
    vidx,
    sidx,
    taps_ref,
    residue_ref,
    decay_ref,
    skip_ref,
    gain_ref,
    spans,
    in_sem,
    small_sem,
    idx_sem,
    halo_send,
    halo_recv,
    state_send,
    state_recv,
    sum_send,
    sum_recv,
    grad_send,
    grad_recv,
):
    n_ctx, n_tp, rows, docs, modes, reach = sizes
    blocks = rows // SUB
    groups = SUB
    total_rows = rows * n_ctx
    width = groups * LANES * n_tp
    me = lax.axis_index("ctx")
    me_tp = lax.axis_index("tp")
    first_row = me * rows
    last_row = first_row + rows - 1
    after = lax.rem(me + 1, n_ctx)
    before = lax.rem(me + n_ctx - 1, n_ctx)

    barrier = pltpu.get_barrier_semaphore()
    for d in range(1, n_ctx):
        pl.semaphore_signal(
            barrier, inc=1, device_id={"ctx": lax.rem(me + d, n_ctx)}, device_id_type=MESH
        )
    for d in range(1, n_tp):
        pl.semaphore_signal(
            barrier, inc=1, device_id={"tp": lax.rem(me_tp + d, n_tp)}, device_id_type=MESH
        )

    small = [
        pltpu.make_async_copy(src, dst, small_sem.at[i])
        for i, (src, dst) in enumerate(
            (
                (spans_hbm, spans),
                (decay_hbm, decay_ref),
                (residue_hbm, residue_ref),
                (taps_hbm, taps_ref),
                (gain_hbm, gain_ref),
                (skip_hbm, skip_ref),
            )
        )
    ]
    for copy in small:
        copy.start()
    loads = [
        pltpu.make_async_copy(src, dst, in_sem.at[i])
        for i, (src, dst) in enumerate(((k_hbm, kb), (v_hbm, vb), (q_hbm, qb), (c_hbm, cb)))
    ]
    for copy in loads:
        copy.start()

    small[0].wait()

    at = first_row + (
        lax.broadcasted_iota(jnp.int32, (SUB, LANES), 0) * LANES
        + lax.broadcasted_iota(jnp.int32, (SUB, LANES), 1)
    )
    begin_v = jnp.zeros((SUB, LANES), jnp.int32)
    for d in range(1, docs):
        start = spans[0, d]
        begin_v = jnp.where(start <= at, jnp.maximum(begin_v, start), begin_v)
    end_v = jnp.full((SUB, LANES), total_rows, jnp.int32)
    for d in range(docs - 1):
        finish = spans[1, d]
        end_v = jnp.where(finish > at, jnp.minimum(end_v, finish), end_v)
    back_taps = jnp.minimum(at - begin_v, reach)
    ahead_taps = jnp.minimum(end_v - 1 - at, reach)
    vidx[0] = back_taps * (3 * (reach + 1))
    vidx[1] = jnp.minimum(back_taps, 1) * modes
    vidx[2] = jnp.minimum(ahead_taps, 1) * modes
    idx_copy = pltpu.make_async_copy(vidx, sidx, idx_sem)
    idx_copy.start()

    b_first = scalar_first(spans, docs, first_row)
    e_first = scalar_end(spans, docs, first_row, total_rows)
    b_last = scalar_first(spans, docs, last_row)
    e_last = scalar_end(spans, docs, last_row, total_rows)
    open_front = jnp.where(b_first < first_row, e_first - first_row, 0)
    open_back = jnp.where(e_last > last_row + 1, b_last - first_row, rows)
    tail_from = b_last - first_row
    head_to = e_first - first_row

    depth = lax.broadcasted_iota(jnp.int32, (SUB, LANES), 0)

    def fill_masks(b, _):
        t = depth + b * SUB
        at_b = pl.ds(pl.multiple_of(b * SUB, SUB), SUB)
        one, none = jnp.ones((SUB, LANES), F32), jnp.zeros((SUB, LANES), F32)
        in_tail[at_b, :] = jnp.where(t >= tail_from, one, none)
        in_head[at_b, :] = jnp.where(t < head_to, one, none)
        in_front[at_b, :] = jnp.where(t < open_front, one, none)
        in_back[at_b, :] = jnp.where(t >= open_back, one, none)
        return 0

    lax.fori_loop(0, blocks, fill_masks, 0)

    for copy in small[1:]:
        copy.wait()

    def spread(src, count, base):
        for g in range(groups):
            ptmp[pl.ds(g * SUB, count), :] = src[:, g * LANES : (g + 1) * LANES]
        return [ptmp[pl.ds(s, SUB, stride=SUB), :] for s in range(count)]

    DEC, AMP, FAR, JUMP = 0, modes, 2 * modes, 3 * modes
    for half in range(modes // SUB):
        cols = spread(decay_ref.at[pl.ds(half * SUB, SUB), :], SUB, 0)
        ress = spread(residue_ref.at[pl.ds(half * SUB, SUB), :], SUB, 0)
        for s in range(SUB):
            r = half * SUB + s
            decay = cols[s] / total_rows
            par[AMP + r] = ress[s] * jnp.sqrt(decay)
            factor = jnp.exp(-decay)
            par[DEC + r] = factor
            par[FAR + r] = jnp.exp(-decay * (rows - SUB))
            par[JUMP + r] = jnp.exp(-decay * rows)
            ft[r] = jnp.zeros((SUB, LANES), F32)
            ft[modes + r] = factor
    for stream in range(3):
        taps = spread(taps_ref.at[stream], reach + 1, 0)
        for pattern in range(reach + 1):
            for j in range(reach + 1):
                wt[(pattern * 3 + stream) * (reach + 1) + j] = (
                    taps[j] if j <= pattern else jnp.zeros((SUB, LANES), F32)
                )
    for g in range(groups):
        gaint[pl.ds(g * SUB, SUB), :] = jnp.broadcast_to(gain_ref[g : g + 1, :], (SUB, LANES))

    pl.semaphore_wait(barrier, n_ctx - 1 + n_tp - 1)

    halo_copies = []
    for i, src in enumerate((k_hbm, v_hbm, q_hbm)):
        copy = pltpu.make_async_remote_copy(
            src_ref=src.at[pl.ds(rows - 16, 16), :],
            dst_ref=halo.at[i],
            send_sem=halo_send.at[i],
            recv_sem=halo_recv.at[i],
            device_id={"ctx": after},
            device_id_type=MESH,
        )
        copy.start()
        halo_copies.append(copy)

    def lift(src, dst):
        def body(i, _):
            for g in range(groups):
                both = src[
                    pl.ds(pl.multiple_of(i * 16, 16), 16), g * LANES : (g + 1) * LANES
                ].astype(F32)
                for h in range(2):
                    dst[
                        pl.ds(
                            pl.multiple_of(((2 * i + 2 + h) * groups + g) * SUB, SUB), SUB
                        ),
                        :,
                    ] = both[h * SUB : (h + 1) * SUB]
            return 0

        lax.fori_loop(0, rows // 16, body, 0)

    def lift_halo(src, dst):
        for g in range(groups):
            both = src[:, g * LANES : (g + 1) * LANES].astype(F32)
            for h in range(2):
                dst[pl.ds((h * groups + g) * SUB, SUB), :] = both[h * SUB : (h + 1) * SUB]

    def offsets(which, b):
        high = lax.div(b, LANES // SUB)
        low = lax.rem(b, LANES // SUB) * SUB
        return [sidx[which, high, low + s] for s in range(SUB)]

    def fir_rows(src, stream, b, patterns):
        xs = [turned(src, b + 1, s) for s in range(SUB - reach, SUB)]
        xs += [turned(src, b + 2, s) for s in range(SUB)]
        out = []
        for s in range(SUB):
            terms = [
                wt[patterns[s] + (stream * (reach + 1) + j)] * xs[s + reach - j] for j in range(reach + 1)
            ]
            out.append(tree_sum(terms))
        return out

    def featurize_kv(b):
        patterns = offsets(0, jnp.int32(b))
        ks = fir_rows(flk, 1, b, patterns)
        vs = fir_rows(flv, 2, b, patterns)
        for s in range(SUB):
            t = b * SUB + s
            put_row(fk, t, ks[s])
            put_row(fv, t, vs[s])
            put_row(inner, t, ks[s] * vs[s])

    def featurize_q(b):
        patterns = offsets(0, jnp.int32(b))
        qs = fir_rows(flq, 0, b, patterns)
        for s in range(SUB):
            put_row(fq, b * SUB + s, qs[s])

    def loop(lo, hi, step):
        def body(i, _):
            step(i)
            return 0

        lax.fori_loop(lo, hi, body, 0)

    loads[0].wait()
    lift(kb, flk)
    loads[1].wait()
    lift(vb, flv)
    idx_copy.wait()
    loop(1, blocks, featurize_kv)

    factors = [par[DEC + r] for r in range(modes)]
    zeros = tuple(jnp.zeros((SUB, LANES), F32) for _ in range(modes))

    def end_rows(source, states, b, forward, keep):
        states = list(states)
        order = range(SUB) if forward else range(SUB - 1, -1, -1)
        for s in order:
            t = b * SUB + s
            x = row(source, t)
            x = x * keep[pl.ds(t, SUB, stride=0), :]
            states = [f * st + x for f, st in zip(factors, states)]
        return tuple(states)

    ends = lax.fori_loop(
        1, blocks, lambda b, st: end_rows(inner, st, b, True, in_tail), zeros
    )
    for copy in halo_copies:
        copy.wait()
    lift_halo(halo.at[0], flk)
    lift_halo(halo.at[1], flv)
    lift_halo(halo.at[2], flq)
    featurize_kv(0)
    heads = end_rows(inner, zeros, 0, True, in_tail)
    for r in range(modes):
        s1tx[0, r] = ends[r] + par[FAR + r] * heads[r]

    def send_all(direction, phase, src, dst):
        copies = []
        for d in range(1, n_ctx):
            target = lax.rem(me + d, n_ctx)
            copy = pltpu.make_async_remote_copy(
                src_ref=src.at[direction, target],
                dst_ref=dst.at[direction, me],
                send_sem=state_send.at[direction, phase, d],
                recv_sem=state_recv.at[direction, phase, d],
                device_id={"ctx": target},
                device_id_type=MESH,
            )
            copy.start()
            copies.append(copy)
        return copies

    def fold(direction):
        jump = par[JUMP + me]
        state = jnp.zeros((SUB, LANES), F32)
        order = range(n_ctx) if direction == 0 else range(n_ctx - 1, -1, -1)
        for i in order:
            s2tx[direction, i] = state
            lo = i * rows
            if direction == 0:
                through = scalar_first(spans, docs, lo + rows - 1) < lo
            else:
                through = scalar_end(spans, docs, lo, total_rows) > lo + rows
            flag = jnp.where(through, jnp.float32(1.0), jnp.float32(0.0))
            state = (jump * flag) * state + s1rx[direction, i]

    def scan_rows(source, states, b, forward, store):
        states = list(states)
        order = range(SUB) if forward else range(SUB - 1, -1, -1)
        keeps = offsets(1 if forward else 2, b)
        for s in order:
            t = b * SUB + s
            x = row(source, t)
            states = [
                ft[keeps[s] + r] * st + x for r, st in enumerate(states)
            ]
            y = tree_sum([a * st for a, st in zip(amps, states)])
            store(t, y + skip * x)
        return tuple(states)

    amps = [par[AMP + r] for r in range(modes)]
    skip = skip_ref[...]

    sent = send_all(0, 0, s1tx, s1rx)

    loads[2].wait()
    lift(qb, flq)
    loop(0, blocks, featurize_q)
    loads[3].wait()

    def lift_cot(i, _):
        for g in range(groups):
            both = cb[pl.ds(pl.multiple_of(i * 16, 16), 16), g * LANES : (g + 1) * LANES].astype(
                F32
            )
            for h in range(2):
                flc[
                    pl.ds(pl.multiple_of(((2 * i + h) * groups + g) * SUB, SUB), SUB), :
                ] = both[h * SUB : (h + 1) * SUB] * gaint[pl.ds(g * SUB, SUB), :]
        return 0

    lax.fori_loop(0, rows // 16, lift_cot, 0)

    for copy in sent:
        copy.wait()
    s1rx[0, me] = s1tx[0, me]
    fold(0)
    sent = send_all(0, 1, s2tx, s2rx)
    lax.fori_loop(
        0,
        blocks,
        lambda b, st: scan_rows(
            inner, st, b, True, lambda t, y: put_row(mix, t, y)
        ),
        zeros,
    )
    for copy in sent:
        copy.wait()
    s2rx[0, me] = s2tx[0, me]

    def correct(b, incs):
        incs = list(incs)
        for s in range(SUB):
            t = b * SUB + s
            incs = [f * c for f, c in zip(factors, incs)]
            m = row(mix, t) + in_front[pl.ds(t, SUB, stride=0), :] * tree_sum(incs)
            put_row(mix, t, m)
            put_row(gated, t, m * row(fq, t))
        return tuple(incs)

    lax.fori_loop(
        0, blocks, correct, tuple(amps[r] * s2rx[0, r] for r in range(modes))
    )

    lane = lax.broadcasted_iota(jnp.int32, (SUB, LANES), 1)

    def row_sums(i, acc):
        for h in range(4):
            acc = block_sums(i * 4 + h, acc)
        return acc

    def block_sums(b, acc):
        gs = [turned(gated, b, g) for g in range(groups)]
        ws = [row(flc, b * groups + g) for g in range(groups)]
        squares = tree_sum([g * g for g in gs])
        cross = tree_sum([g * w for g, w in zip(gs, ws)])
        acc = jnp.where(lane == b, jnp.sum(squares, axis=1, keepdims=True), acc)
        return jnp.where(lane == b + blocks, jnp.sum(cross, axis=1, keepdims=True), acc)

    sums_tx[...] = lax.fori_loop(0, blocks // 4, row_sums, jnp.zeros((SUB, LANES), F32))
    sent = []
    for d in range(1, n_tp):
        copy = pltpu.make_async_remote_copy(
            src_ref=sums_tx,
            dst_ref=sums_rx.at[me_tp],
            send_sem=sum_send.at[d],
            recv_sem=sum_recv.at[d],
            device_id={"tp": lax.rem(me_tp + d, n_tp)},
            device_id_type=MESH,
        )
        copy.start()
        sent.append(copy)
    for copy in sent:
        copy.wait()
    sums_rx[me_tp] = sums_tx[...]
    total = tree_sum([sums_rx[i] for i in range(n_tp)])
    inv_rms = lax.rsqrt(total / width + 1e-6)
    cross = pltpu.roll(total, LANES - blocks, 1)
    cubed = inv_rms * inv_rms * inv_rms * cross / width
    for b in range(blocks):
        alpha[pl.ds(b * SUB, SUB), :] = jnp.broadcast_to(inv_rms[:, b : b + 1], (SUB, LANES))
        beta[pl.ds(b * SUB, SUB), :] = jnp.broadcast_to(cubed[:, b : b + 1], (SUB, LANES))

    def grads(i, states):
        b = blocks - 1 - i
        for s in range(SUB):
            t = b * SUB + s
            al = alpha[pl.ds(t, SUB, stride=0), :]
            be = beta[pl.ds(t, SUB, stride=0), :]
            grad = al * turned(flc, b, s) - be * row(gated, t)
            put_row(gradq, t, grad * row(mix, t))
            put_row(gmix, t, grad * row(fq, t))
        return end_rows(gmix, states, b, False, in_head)

    ends = lax.fori_loop(0, blocks, grads, zeros)
    for r in range(modes):
        s1tx[1, r] = ends[r]
    sent = send_all(1, 0, s1tx, s1rx)

    def send_halo(i, src):
        copy = pltpu.make_async_remote_copy(
            src_ref=src.at[pl.ds(0, SUB * SUB), :],
            dst_ref=ghalo.at[i],
            send_sem=grad_send.at[i],
            recv_sem=grad_recv.at[i],
            device_id={"ctx": before},
            device_id_type=MESH,
        )
        copy.start()
        return copy

    grad_copies = [send_halo(0, gradq)]

    for copy in sent:
        copy.wait()
    s1rx[1, me] = s1tx[1, me]
    fold(1)
    sent = send_all(1, 1, s2tx, s2rx)

    lax.fori_loop(
        0,
        blocks,
        lambda i, st: scan_rows(
            gmix, st, blocks - 1 - i, False, lambda t, y: put_row(back, t, y)
        ),
        zeros,
    )

    for copy in sent:
        copy.wait()
    s2rx[1, me] = s2tx[1, me]

    def correct_back(b, incs):
        incs = list(incs)
        for s in range(SUB - 1, -1, -1):
            t = b * SUB + s
            incs = [f * c for f, c in zip(factors, incs)]
            grad = row(back, t) + in_back[pl.ds(t, SUB, stride=0), :] * tree_sum(incs)
            put_row(gradk, t, grad * row(fv, t))
            put_row(gradv, t, grad * row(fk, t))
        return tuple(incs)

    incs = tuple(amps[r] * s2rx[1, r] for r in range(modes))
    correct_back(0, tuple(par[FAR + r] * incs[r] for r in range(modes)))
    grad_copies.append(send_halo(1, gradk))
    grad_copies.append(send_halo(2, gradv))
    lax.fori_loop(0, blocks - 1, lambda i, c: correct_back(blocks - 1 - i, c), incs)
    for i, dst in enumerate((gradq, gradk, gradv)):
        grad_copies[i].wait()
        for r in range(SUB):
            dst[pl.ds((rows + r) * SUB, SUB), :] = ghalo[i, pl.ds(r * SUB, SUB), :]


def finish(
    sizes,
    gradq,
    gradk,
    gradv,
    gated,
    alpha,
    taps_hbm,
    gain_hbm,
    spans_hbm,
    mixed_hbm,
    gq_hbm,
    gk_hbm,
    gv_hbm,
    taps_ref,
    gain_ref,
    spans,
    small_sem,
    stage,
    ob,
    ptmp,
    out_sem,
):
    n_ctx, n_tp, rows, docs, modes, reach = sizes
    blocks, groups = rows // SUB, SUB
    first_row = lax.axis_index("ctx") * rows

    small = [
        pltpu.make_async_copy(src, dst, small_sem.at[i])
        for i, (src, dst) in enumerate(
            ((gain_hbm, gain_ref), (taps_hbm, taps_ref), (spans_hbm, spans))
        )
    ]
    for copy in small:
        copy.start()
    for copy in small:
        copy.wait()

    def emit(slot, half, dst):
        part = pl.ds(half * (rows // 2), rows // 2)
        copy = pltpu.make_async_copy(
            ob.at[slot, part, :], dst.at[part, :], out_sem.at[slot, half]
        )
        copy.start()
        return copy

    def put_pair(slot, i, g, low, high):
        both = jnp.concatenate([low, high], axis=0)
        ob[slot, pl.ds(pl.multiple_of(i * 16, 16), 16), g * LANES : (g + 1) * LANES] = (
            both.astype(jnp.bfloat16)
        )

    def lower_mixed(i, _):
        for g in range(groups):
            gain = jnp.broadcast_to(gain_ref[g : g + 1, :], (SUB, LANES))
            halves = []
            for h in range(2):
                b = 2 * i + h
                al = alpha[pl.ds(pl.multiple_of(b * SUB, SUB), SUB), :]
                halves.append(turned(gated, b, g) * al * gain)
            put_pair(0, i, g, *halves)
        return 0

    outs = []
    for half in range(2):
        lax.fori_loop(half * rows // 32, (half + 1) * rows // 32, lower_mixed, 0)
        outs.append(emit(0, half, mixed_hbm))

    def lower(i, slot):
        for g in range(groups):
            put_pair(slot, i, g, turned(stage, 2 * i, g), turned(stage, 2 * i + 1, g))
        return slot

    for stream, (src, dst) in enumerate(((gradq, gq_hbm), (gradk, gk_hbm), (gradv, gv_hbm))):
        for g in range(groups):
            ptmp[pl.ds(g * SUB, reach + 1), :] = taps_ref[
                stream, :, g * LANES : (g + 1) * LANES
            ]
        taps = [ptmp[pl.ds(s, SUB, stride=SUB), :] for s in range(reach + 1)]

        def step(b, _):
            first = first_row + b * SUB
            crossed = jnp.bool_(False)
            for d in range(docs):
                finish_at = spans[1, d]
                crossed = crossed | ((finish_at > first) & (finish_at < first + SUB + reach))
            xs = [row(src, b * SUB + s) for s in range(SUB + reach)]

            @pl.when(jnp.logical_not(crossed))
            def _():
                for s in range(SUB):
                    terms = [taps[j] * xs[s + j] for j in range(reach + 1)]
                    put_row(stage, b * SUB + s, tree_sum(terms))

            @pl.when(crossed)
            def _():
                for s in range(SUB):
                    end = scalar_end(spans, docs, first + s, rows * n_ctx)
                    terms = []
                    for j in range(reach + 1):
                        inside = jnp.where(first + s + j < end, 1.0, 0.0)
                        terms.append(taps[j] * (inside * xs[s + j]))
                    put_row(stage, b * SUB + s, tree_sum(terms))

            return 0

        for half in range(2):
            lax.fori_loop(half * blocks // 2, (half + 1) * blocks // 2, step, 0)
            lax.fori_loop(half * rows // 32, (half + 1) * rows // 32, lower, 1 + stream)
            outs.append(emit(1 + stream, half, dst))
    for copy in outs:
        copy.wait()


def solution(mesh):
    n_ctx, n_tp = mesh.shape["ctx"], mesh.shape["tp"]

    def local(q, k, v, taps, residue, decay, skip, gain, spans, cot):
        rows, cols = q.shape
        modes, docs, reach = residue.shape[0], spans.shape[0], taps.shape[1] - 1
        assert cols == SUB * LANES and modes == n_ctx and rows % 16 == 0
        assert rows // SUB * 2 <= LANES and rows <= SUB * LANES and modes % SUB == 0
        flat = (rows * SUB, LANES)
        front = ((rows + 16) * SUB, LANES)
        tail = ((rows + SUB) * SUB, LANES)
        V = pltpu.VMEM
        D = pltpu.SemaphoreType.DMA
        tile = (SUB, LANES)
        scratch = (
            [V((rows, cols), jnp.bfloat16)] * 4
            + [V((3, 16, cols), jnp.bfloat16)]
            + [V(front, F32)] * 3
            + [V(flat, F32)] * 8
            + [V((3, SUB * SUB, LANES), F32)]
            + [
                V(((reach + 1) * 3 * (reach + 1),) + tile, F32),
                V((2 * modes,) + tile, F32),
                V((4 * modes,) + tile, F32),
                V((SUB * SUB, LANES), F32),
                V((SUB * SUB, LANES), F32),
            ]
            + [V((rows + SUB, LANES), F32)] * 5
            + [
                V(tile, F32),
                V((n_tp,) + tile, F32),
                V((2, n_ctx) + tile, F32),
                V((2, n_ctx) + tile, F32),
                V((2, n_ctx) + tile, F32),
                V((2, n_ctx) + tile, F32),
                V((3,) + tile, jnp.int32),
                pltpu.SMEM((3,) + tile, jnp.int32),
                V((3, reach + 1, cols), F32),
                V((modes, cols), F32),
                V((modes, cols), F32),
                V(tile, F32),
                V(tile, F32),
                pltpu.SMEM((2, docs), jnp.int32),
                D((4,)),
                D((6,)),
                D,
                D((3,)),
                D((3,)),
                D((2, 2, n_ctx)),
                D((2, 2, n_ctx)),
                D((n_tp,)),
                D((n_tp,)),
                D((3,)),
                D((3,)),
            ]
        )
        hbm = pl.BlockSpec(memory_space=pltpu.HBM)
        vmem = pl.BlockSpec(memory_space=pltpu.VMEM)
        out = jax.ShapeDtypeStruct((rows, cols), jnp.bfloat16)
        sizes = (n_ctx, n_tp, rows, docs, modes, reach)
        smem = pl.BlockSpec(memory_space=pltpu.SMEM)
        gain, spans = gain.reshape(SUB, LANES), spans.T
        held = [jax.ShapeDtypeStruct(tail, F32)] * 3
        held += [jax.ShapeDtypeStruct(flat, F32), jax.ShapeDtypeStruct((rows + SUB, LANES), F32)]
        args = (q, k, v, cot, taps, residue, decay, skip.reshape(SUB, LANES), gain, spans)
        args = [pltpu.with_memory_space_constraint(a, pltpu.HBM) for a in args]
        parts = pl.pallas_call(
            functools.partial(kernel, sizes),
            out_shape=held,
            in_specs=[hbm] * 10,
            out_specs=[vmem] * 5,
            scratch_shapes=scratch,
            compiler_params=pltpu.CompilerParams(
                collective_id=0, has_side_effects=True, vmem_limit_bytes=GRANT
            ),
            name="hyena",
        )(*args)
        return pl.pallas_call(
            functools.partial(finish, sizes),
            out_shape=(out,) * 4,
            in_specs=[vmem] * 5 + [hbm] * 3,
            out_specs=(hbm,) * 4,
            scratch_shapes=[
                V((3, reach + 1, cols), F32),
                V(tile, F32),
                pltpu.SMEM((2, docs), jnp.int32),
                D((3,)),
                V(flat, F32),
                V((4, rows, cols), jnp.bfloat16),
                V((SUB * SUB, LANES), F32),
                D((4, 2)),
            ],
            compiler_params=pltpu.CompilerParams(vmem_limit_bytes=LAST_GRANT),
            name="finish",
        )(*parts, args[4], args[8], args[9])

    placed = (
        P("ctx", "tp"),
        P("ctx", "tp"),
        P("ctx", "tp"),
        P(None, None, "tp"),
        P(None, "tp"),
        P(None, "tp"),
        P("tp"),
        P("tp"),
        P(),
        P("ctx", "tp"),
    )
    return jax.shard_map(
        local,
        mesh=mesh,
        in_specs=placed,
        out_specs=(P("ctx", "tp"),) * 4,
        check_vma=False,
    )
```

```python
import functools

import jax
import jax.numpy as jnp
from jax import lax
from jax.experimental import pallas as pl
from jax.experimental.pallas import tpu as pltpu
from jax.sharding import PartitionSpec as P

MESH = pl.DeviceIdType.MESH
F32 = jnp.float32
LANES = 128
SUB = 8
GRANT = 40 * 1024 * 1024
LAST_GRANT = 20 * 1024 * 1024
FRONT_CUT = 8
BACK_CUT = 16


def tree_sum(terms):
    while len(terms) > 1:
        paired = [terms[i] + terms[i + 1] for i in range(0, len(terms) - 1, 2)]
        if len(terms) % 2:
            paired.append(terms[-1])
        terms = paired
    return terms[0]


def row(ref, t):
    return ref[pl.ds(pl.multiple_of(t * SUB, SUB), SUB), :]


def put_row(ref, t, value):
    ref[pl.ds(pl.multiple_of(t * SUB, SUB), SUB), :] = value


def turned(ref, block, s):
    return ref[pl.ds(block * SUB * SUB + s, SUB, stride=SUB), :]


def scalar_first(spans, docs, t):
    first = jnp.int32(0)
    for d in range(1, docs):
        start = spans[0, d]
        first = jnp.where(start <= t, jnp.maximum(first, start), first)
    return first


def scalar_end(spans, docs, t, total):
    end = jnp.int32(total)
    for d in range(docs - 1):
        finish = spans[1, d]
        end = jnp.where(finish > t, jnp.minimum(end, finish), end)
    return end


def kernel(
    sizes,
    q_hbm,
    k_hbm,
    v_hbm,
    c_hbm,
    taps_hbm,
    residue_hbm,
    decay_hbm,
    skip_hbm,
    gain_hbm,
    spans_hbm,
    gradq,
    gradk,
    gradv,
    gated,
    alpha,
    qb,
    kb,
    vb,
    cb,
    halo,
    flq,
    flk,
    flv,
    flc,
    fq,
    fk,
    fv,
    inner,
    mix,
    gmix,
    back,
    ghalo,
    wt,
    ft,
    par,
    ptmp,
    gaint,
    beta,
    in_tail,
    in_head,
    in_front,
    in_back,
    sums_tx,
    sums_rx,
    s1tx,
    s1rx,
    s2tx,
    s2rx,
    vidx,
    sidx,
    taps_ref,
    residue_ref,
    decay_ref,
    skip_ref,
    gain_ref,
    spans,
    in_sem,
    small_sem,
    idx_sem,
    halo_send,
    halo_recv,
    state_send,
    state_recv,
    sum_send,
    sum_recv,
    grad_send,
    grad_recv,
):
    n_ctx, n_tp, rows, docs, modes, reach = sizes
    blocks = rows // SUB
    groups = SUB
    total_rows = rows * n_ctx
    width = groups * LANES * n_tp
    me = lax.axis_index("ctx")
    me_tp = lax.axis_index("tp")
    first_row = me * rows
    last_row = first_row + rows - 1
    after = lax.rem(me + 1, n_ctx)
    before = lax.rem(me + n_ctx - 1, n_ctx)

    barrier = pltpu.get_barrier_semaphore()
    for d in range(1, n_ctx):
        pl.semaphore_signal(
            barrier, inc=1, device_id={"ctx": lax.rem(me + d, n_ctx)}, device_id_type=MESH
        )
    for d in range(1, n_tp):
        pl.semaphore_signal(
            barrier, inc=1, device_id={"tp": lax.rem(me_tp + d, n_tp)}, device_id_type=MESH
        )

    small = [
        pltpu.make_async_copy(src, dst, small_sem.at[i])
        for i, (src, dst) in enumerate(
            (
                (spans_hbm, spans),
                (decay_hbm, decay_ref),
                (residue_hbm, residue_ref),
                (taps_hbm, taps_ref),
                (gain_hbm, gain_ref),
                (skip_hbm, skip_ref),
            )
        )
    ]
    for copy in small:
        copy.start()
    loads = [
        pltpu.make_async_copy(src, dst, in_sem.at[i])
        for i, (src, dst) in enumerate(((k_hbm, kb), (v_hbm, vb), (q_hbm, qb), (c_hbm, cb)))
    ]
    for copy in loads:
        copy.start()

    small[0].wait()

    at = first_row + (
        lax.broadcasted_iota(jnp.int32, (SUB, LANES), 0) * LANES
        + lax.broadcasted_iota(jnp.int32, (SUB, LANES), 1)
    )
    begin_v = jnp.zeros((SUB, LANES), jnp.int32)
    for d in range(1, docs):
        start = spans[0, d]
        begin_v = jnp.where(start <= at, jnp.maximum(begin_v, start), begin_v)
    end_v = jnp.full((SUB, LANES), total_rows, jnp.int32)
    for d in range(docs - 1):
        finish = spans[1, d]
        end_v = jnp.where(finish > at, jnp.minimum(end_v, finish), end_v)
    back_taps = jnp.minimum(at - begin_v, reach)
    ahead_taps = jnp.minimum(end_v - 1 - at, reach)
    vidx[0] = back_taps * (3 * (reach + 1))
    vidx[1] = jnp.minimum(back_taps, 1) * modes
    vidx[2] = jnp.minimum(ahead_taps, 1) * modes
    idx_copy = pltpu.make_async_copy(vidx, sidx, idx_sem)
    idx_copy.start()

    b_first = scalar_first(spans, docs, first_row)
    e_first = scalar_end(spans, docs, first_row, total_rows)
    b_last = scalar_first(spans, docs, last_row)
    e_last = scalar_end(spans, docs, last_row, total_rows)
    open_front = jnp.where(b_first < first_row, e_first - first_row, 0)
    open_back = jnp.where(e_last > last_row + 1, b_last - first_row, rows)
    tail_from = b_last - first_row
    head_to = e_first - first_row

    depth = lax.broadcasted_iota(jnp.int32, (SUB, LANES), 0)

    def fill_masks(b, _):
        t = depth + b * SUB
        at_b = pl.ds(pl.multiple_of(b * SUB, SUB), SUB)
        one, none = jnp.ones((SUB, LANES), F32), jnp.zeros((SUB, LANES), F32)
        in_tail[at_b, :] = jnp.where(t >= tail_from, one, none)
        in_head[at_b, :] = jnp.where(t < head_to, one, none)
        in_front[at_b, :] = jnp.where(t < open_front, one, none)
        in_back[at_b, :] = jnp.where(t >= open_back, one, none)
        return 0

    lax.fori_loop(0, blocks, fill_masks, 0)

    for copy in small[1:]:
        copy.wait()

    def spread(src, count, base):
        for g in range(groups):
            ptmp[pl.ds(g * SUB, count), :] = src[:, g * LANES : (g + 1) * LANES]
        return [ptmp[pl.ds(s, SUB, stride=SUB), :] for s in range(count)]

    DEC, AMP, FAR, JUMP, MID = (i * modes for i in range(5))
    for half in range(modes // SUB):
        cols = spread(decay_ref.at[pl.ds(half * SUB, SUB), :], SUB, 0)
        ress = spread(residue_ref.at[pl.ds(half * SUB, SUB), :], SUB, 0)
        for s in range(SUB):
            r = half * SUB + s
            decay = cols[s] / total_rows
            par[AMP + r] = ress[s] * jnp.sqrt(decay)
            factor = jnp.exp(-decay)
            par[DEC + r] = factor
            par[FAR + r] = jnp.exp(-decay * (rows - SUB))
            par[MID + r] = jnp.exp(-decay * (rows // 2))
            par[JUMP + r] = jnp.exp(-decay * rows)
            ft[r] = jnp.zeros((SUB, LANES), F32)
            ft[modes + r] = factor
    for stream in range(3):
        taps = spread(taps_ref.at[stream], reach + 1, 0)
        for pattern in range(reach + 1):
            for j in range(reach + 1):
                wt[(pattern * 3 + stream) * (reach + 1) + j] = (
                    taps[j] if j <= pattern else jnp.zeros((SUB, LANES), F32)
                )
    for g in range(groups):
        gaint[pl.ds(g * SUB, SUB), :] = jnp.broadcast_to(gain_ref[g : g + 1, :], (SUB, LANES))

    def lift(src, dst):
        def body(i, _):
            for g in range(groups):
                both = src[
                    pl.ds(pl.multiple_of(i * 16, 16), 16), g * LANES : (g + 1) * LANES
                ].astype(F32)
                for h in range(2):
                    dst[
                        pl.ds(
                            pl.multiple_of(((2 * i + 2 + h) * groups + g) * SUB, SUB), SUB
                        ),
                        :,
                    ] = both[h * SUB : (h + 1) * SUB]
            return 0

        lax.fori_loop(0, rows // 16, body, 0)

    def lift_halo(src, dst):
        for g in range(groups):
            both = src[:, g * LANES : (g + 1) * LANES].astype(F32)
            for h in range(2):
                dst[pl.ds((h * groups + g) * SUB, SUB), :] = both[h * SUB : (h + 1) * SUB]

    def offsets(which, b):
        high = lax.div(b, LANES // SUB)
        low = lax.rem(b, LANES // SUB) * SUB
        return [sidx[which, high, low + s] for s in range(SUB)]

    def fir_rows(src, stream, b, count, patterns):
        xs = [turned(src, b + 1, s) for s in range(SUB - reach, SUB)]
        for h in range(count):
            xs += [turned(src, b + 2 + h, s) for s in range(SUB)]
        out = []
        for s in range(SUB * count):
            terms = [
                wt[patterns[s] + (stream * (reach + 1) + j)] * xs[s + reach - j] for j in range(reach + 1)
            ]
            out.append(tree_sum(terms))
        return out

    def featurize_kv(b, count):
        patterns = [p for h in range(count) for p in offsets(0, jnp.int32(b + h))]
        ks = fir_rows(flk, 1, b, count, patterns)
        vs = fir_rows(flv, 2, b, count, patterns)
        for s in range(SUB * count):
            t = b * SUB + s
            put_row(fk, t, ks[s])
            put_row(fv, t, vs[s])
            put_row(inner, t, ks[s] * vs[s])

    def featurize_q(b, count):
        patterns = [p for h in range(count) for p in offsets(0, jnp.int32(b + h))]
        qs = fir_rows(flq, 0, b, count, patterns)
        for s in range(SUB * count):
            put_row(fq, b * SUB + s, qs[s])

    def loop(lo, hi, step):
        def body(i, _):
            step(i)
            return 0

        lax.fori_loop(lo, hi, body, 0)

    loads[0].wait()
    lift(kb, flk)
    loads[1].wait()
    lift(vb, flv)
    pl.semaphore_wait(barrier, n_ctx - 1 + n_tp - 1)

    halo_copies = []
    for i, src in enumerate((k_hbm, v_hbm, q_hbm)):
        copy = pltpu.make_async_remote_copy(
            src_ref=src.at[pl.ds(rows - 16, 16), :],
            dst_ref=halo.at[i],
            send_sem=halo_send.at[i],
            recv_sem=halo_recv.at[i],
            device_id={"ctx": after},
            device_id_type=MESH,
        )
        copy.start()
        halo_copies.append(copy)

    idx_copy.wait()
    featurize_kv(1, 1)
    loop(1, blocks // 2, lambda i: featurize_kv(2 * i, 2))

    factors = [par[DEC + r] for r in range(modes)]
    zeros = tuple(jnp.zeros((SUB, LANES), F32) for _ in range(modes))

    def end_rows(source, states, b, forward, keep):
        states = list(states)
        order = range(SUB) if forward else range(SUB - 1, -1, -1)
        for s in order:
            t = b * SUB + s
            x = row(source, t)
            x = x * keep[pl.ds(t, SUB, stride=0), :]
            states = [f * st + x for f, st in zip(factors, states)]
        return tuple(states)

    ends = lax.fori_loop(
        1, blocks, lambda b, st: end_rows(inner, st, b, True, in_tail), zeros
    )
    for copy in halo_copies:
        copy.wait()
    lift_halo(halo.at[0], flk)
    lift_halo(halo.at[1], flv)
    lift_halo(halo.at[2], flq)
    featurize_kv(0, 1)
    heads = end_rows(inner, zeros, 0, True, in_tail)
    for r in range(modes):
        s1tx[0, r] = ends[r] + par[FAR + r] * heads[r]

    def send_all(direction, phase, src, dst):
        copies = []
        for d in range(1, n_ctx):
            target = lax.rem(me + d, n_ctx)
            copy = pltpu.make_async_remote_copy(
                src_ref=src.at[direction, target],
                dst_ref=dst.at[direction, me],
                send_sem=state_send.at[direction, phase, d],
                recv_sem=state_recv.at[direction, phase, d],
                device_id={"ctx": target},
                device_id_type=MESH,
            )
            copy.start()
            copies.append(copy)
        return copies

    def fold(direction):
        jump = par[JUMP + me]
        state = jnp.zeros((SUB, LANES), F32)
        order = range(n_ctx) if direction == 0 else range(n_ctx - 1, -1, -1)
        for i in order:
            s2tx[direction, i] = state
            lo = i * rows
            if direction == 0:
                through = scalar_first(spans, docs, lo + rows - 1) < lo
            else:
                through = scalar_end(spans, docs, lo, total_rows) > lo + rows
            flag = jnp.where(through, jnp.float32(1.0), jnp.float32(0.0))
            state = (jump * flag) * state + s1rx[direction, i]

    def scan(source, states, lo, hi, forward, dst):
        order = range(SUB) if forward else range(SUB - 1, -1, -1)

        def body(i, states):
            states = list(states)
            for h in range(2):
                b = 2 * i + h if forward else blocks - 1 - 2 * i - h
                keeps = offsets(1 if forward else 2, b)
                for s in order:
                    t = b * SUB + s
                    x = row(source, t)
                    states = [ft[keeps[s] + r] * st + x for r, st in enumerate(states)]
                    y = tree_sum([a * st for a, st in zip(amps, states)])
                    put_row(dst, t, y + skip * x)
            return tuple(states)

        return lax.fori_loop(lo, hi, body, states)

    amps = [par[AMP + r] for r in range(modes)]
    skip = skip_ref[...]

    sent = send_all(0, 0, s1tx, s1rx)

    loads[2].wait()
    lift(qb, flq)
    loop(0, blocks // 2, lambda i: featurize_q(2 * i, 2))
    loads[3].wait()

    def lift_cot(i, _):
        for g in range(groups):
            both = cb[pl.ds(pl.multiple_of(i * 16, 16), 16), g * LANES : (g + 1) * LANES].astype(
                F32
            )
            for h in range(2):
                flc[
                    pl.ds(pl.multiple_of(((2 * i + h) * groups + g) * SUB, SUB), SUB), :
                ] = both[h * SUB : (h + 1) * SUB] * gaint[pl.ds(g * SUB, SUB), :]
        return 0

    lax.fori_loop(0, rows // 16, lift_cot, 0)

    states = scan(inner, zeros, 0, FRONT_CUT, True, mix)
    for copy in sent:
        copy.wait()
    s1rx[0, me] = s1tx[0, me]
    fold(0)
    sent = send_all(0, 1, s2tx, s2rx)
    scan(inner, states, FRONT_CUT, blocks // 2, True, mix)
    for copy in sent:
        copy.wait()
    s2rx[0, me] = s2tx[0, me]

    def correct(b, incs):
        incs = list(incs)
        for s in range(SUB):
            t = b * SUB + s
            incs = [f * c for f, c in zip(factors, incs)]
            m = row(mix, t) + in_front[pl.ds(t, SUB, stride=0), :] * tree_sum(incs)
            put_row(mix, t, m)
            put_row(gated, t, m * row(fq, t))
        return tuple(incs)

    lane = lax.broadcasted_iota(jnp.int32, (SUB, LANES), 1)

    def block_sums(b, acc):
        gs = [turned(gated, b, g) for g in range(groups)]
        ws = [row(flc, b * groups + g) for g in range(groups)]
        squares = tree_sum([g * g for g in gs])
        cross = tree_sum([g * w for g, w in zip(gs, ws)])
        acc = jnp.where(lane == b, jnp.sum(squares, axis=1, keepdims=True), acc)
        return jnp.where(lane == b + blocks, jnp.sum(cross, axis=1, keepdims=True), acc)

    def row_sums(i, acc):
        for h in range(4):
            acc = block_sums(i * 4 + h, acc)
        return acc

    def send_sums(half):
        sums_tx[half] = lax.fori_loop(
            half * blocks // 8,
            (half + 1) * blocks // 8,
            row_sums,
            jnp.zeros((SUB, LANES), F32),
        )
        copies = []
        for d in range(1, n_tp):
            copy = pltpu.make_async_remote_copy(
                src_ref=sums_tx.at[half],
                dst_ref=sums_rx.at[half, me_tp],
                send_sem=sum_send.at[half, d],
                recv_sem=sum_recv.at[half, d],
                device_id={"tp": lax.rem(me_tp + d, n_tp)},
                device_id_type=MESH,
            )
            copy.start()
            copies.append(copy)
        return copies

    incs = [amps[r] * s2rx[0, r] for r in range(modes)]
    lax.fori_loop(
        blocks // 2, blocks, correct, tuple(par[MID + r] * incs[r] for r in range(modes))
    )
    late = send_sums(1)
    lax.fori_loop(0, blocks // 2, correct, tuple(incs))
    early = send_sums(0)

    def take_sums(half, copies):
        for copy in copies:
            copy.wait()
        sums_rx[half, me_tp] = sums_tx[half]
        total = tree_sum([sums_rx[half, i] for i in range(n_tp)])
        inv_rms = lax.rsqrt(total / width + 1e-6)
        cross = pltpu.roll(total, LANES - blocks, 1)
        cubed = inv_rms * inv_rms * inv_rms * cross / width
        for b in range(half * blocks // 2, (half + 1) * blocks // 2):
            at_b = pl.ds(b * SUB, SUB)
            alpha[at_b, :] = jnp.broadcast_to(inv_rms[:, b : b + 1], (SUB, LANES))
            beta[at_b, :] = jnp.broadcast_to(cubed[:, b : b + 1], (SUB, LANES))

    def grads(i, states):
        b = blocks - 1 - i
        for s in range(SUB):
            t = b * SUB + s
            al = alpha[pl.ds(t, SUB, stride=0), :]
            be = beta[pl.ds(t, SUB, stride=0), :]
            grad = al * turned(flc, b, s) - be * row(gated, t)
            put_row(gradq, t, grad * row(mix, t))
            put_row(gmix, t, grad * row(fq, t))
        return end_rows(gmix, states, b, False, in_head)

    take_sums(1, late)
    ends = lax.fori_loop(0, blocks // 2, grads, zeros)
    take_sums(0, early)
    ends = lax.fori_loop(blocks // 2, blocks, grads, ends)
    for r in range(modes):
        s1tx[1, r] = ends[r]
    sent = send_all(1, 0, s1tx, s1rx)

    def send_halo(i, src):
        copy = pltpu.make_async_remote_copy(
            src_ref=src.at[pl.ds(0, SUB * SUB), :],
            dst_ref=ghalo.at[i],
            send_sem=grad_send.at[i],
            recv_sem=grad_recv.at[i],
            device_id={"ctx": before},
            device_id_type=MESH,
        )
        copy.start()
        return copy

    grad_copies = [send_halo(0, gradq)]

    states = scan(gmix, zeros, 0, BACK_CUT, False, back)
    for copy in sent:
        copy.wait()
    s1rx[1, me] = s1tx[1, me]
    fold(1)
    sent = send_all(1, 1, s2tx, s2rx)
    scan(gmix, states, BACK_CUT, blocks // 2, False, back)

    for copy in sent:
        copy.wait()
    s2rx[1, me] = s2tx[1, me]

    def correct_back(b, incs):
        incs = list(incs)
        for s in range(SUB - 1, -1, -1):
            t = b * SUB + s
            incs = [f * c for f, c in zip(factors, incs)]
            grad = row(back, t) + in_back[pl.ds(t, SUB, stride=0), :] * tree_sum(incs)
            put_row(gradk, t, grad * row(fv, t))
            put_row(gradv, t, grad * row(fk, t))
        return tuple(incs)

    incs = tuple(amps[r] * s2rx[1, r] for r in range(modes))
    correct_back(0, tuple(par[FAR + r] * incs[r] for r in range(modes)))
    grad_copies.append(send_halo(1, gradk))
    grad_copies.append(send_halo(2, gradv))
    lax.fori_loop(0, blocks - 1, lambda i, c: correct_back(blocks - 1 - i, c), incs)
    for i, dst in enumerate((gradq, gradk, gradv)):
        grad_copies[i].wait()
        for r in range(SUB):
            dst[pl.ds((rows + r) * SUB, SUB), :] = ghalo[i, pl.ds(r * SUB, SUB), :]


def finish(
    sizes,
    gradq,
    gradk,
    gradv,
    gated,
    alpha,
    taps_hbm,
    gain_hbm,
    spans_hbm,
    mixed_hbm,
    gq_hbm,
    gk_hbm,
    gv_hbm,
    taps_ref,
    gain_ref,
    spans,
    small_sem,
    stage,
    ob,
    ptmp,
    out_sem,
):
    n_ctx, n_tp, rows, docs, modes, reach = sizes
    blocks, groups = rows // SUB, SUB
    first_row = lax.axis_index("ctx") * rows

    small = [
        pltpu.make_async_copy(src, dst, small_sem.at[i])
        for i, (src, dst) in enumerate(
            ((gain_hbm, gain_ref), (taps_hbm, taps_ref), (spans_hbm, spans))
        )
    ]
    for copy in small:
        copy.start()
    for copy in small:
        copy.wait()

    def emit(slot, half, dst):
        part = pl.ds(half * (rows // 2), rows // 2)
        copy = pltpu.make_async_copy(
            ob.at[slot, part, :], dst.at[part, :], out_sem.at[slot, half]
        )
        copy.start()
        return copy

    def put_pair(slot, i, g, low, high):
        both = jnp.concatenate([low, high], axis=0)
        ob[slot, pl.ds(pl.multiple_of(i * 16, 16), 16), g * LANES : (g + 1) * LANES] = (
            both.astype(jnp.bfloat16)
        )

    def lower_mixed(i, _):
        for g in range(groups):
            gain = jnp.broadcast_to(gain_ref[g : g + 1, :], (SUB, LANES))
            halves = []
            for h in range(2):
                b = 2 * i + h
                al = alpha[pl.ds(pl.multiple_of(b * SUB, SUB), SUB), :]
                halves.append(turned(gated, b, g) * al * gain)
            put_pair(0, i, g, *halves)
        return 0

    outs = []
    for half in range(2):
        lax.fori_loop(half * rows // 32, (half + 1) * rows // 32, lower_mixed, 0)
        outs.append(emit(0, half, mixed_hbm))

    def lower(i, slot):
        for g in range(groups):
            put_pair(slot, i, g, turned(stage, 2 * i, g), turned(stage, 2 * i + 1, g))
        return slot

    for stream, (src, dst) in enumerate(((gradq, gq_hbm), (gradk, gk_hbm), (gradv, gv_hbm))):
        for g in range(groups):
            ptmp[pl.ds(g * SUB, reach + 1), :] = taps_ref[
                stream, :, g * LANES : (g + 1) * LANES
            ]
        taps = [ptmp[pl.ds(s, SUB, stride=SUB), :] for s in range(reach + 1)]

        def step(i, _):
            xs = [row(src, i * 2 * SUB + s) for s in range(2 * SUB + reach)]
            for s in range(2 * SUB):
                terms = [taps[j] * xs[s + j] for j in range(reach + 1)]
                put_row(stage, i * 2 * SUB + s, tree_sum(terms))
            return 0

        lax.fori_loop(0, blocks // 2, step, 0)

        for d in range(docs):
            stop = spans[1, d]
            high = (stop - 1 - first_row) // SUB
            for b in (high - 1, high):

                @pl.when((stop > first_row) & (b >= 0) & (b < blocks))
                def _():
                    for s in range(SUB):
                        t = first_row + b * SUB + s
                        end = scalar_end(spans, docs, t, rows * n_ctx)
                        terms = []
                        for j in range(reach + 1):
                            inside = jnp.where(t + j < end, 1.0, 0.0)
                            terms.append(taps[j] * (inside * row(src, b * SUB + s + j)))
                        put_row(stage, b * SUB + s, tree_sum(terms))

        for half in range(2):
            lax.fori_loop(half * rows // 32, (half + 1) * rows // 32, lower, 1 + stream)
            outs.append(emit(1 + stream, half, dst))
    for copy in outs:
        copy.wait()


def solution(mesh):
    n_ctx, n_tp = mesh.shape["ctx"], mesh.shape["tp"]

    def local(q, k, v, taps, residue, decay, skip, gain, spans, cot):
        rows, cols = q.shape
        modes, docs, reach = residue.shape[0], spans.shape[0], taps.shape[1] - 1
        assert cols == SUB * LANES and modes == n_ctx and rows % 16 == 0
        assert rows // SUB * 2 <= LANES and rows <= SUB * LANES and modes % SUB == 0
        flat = (rows * SUB, LANES)
        front = ((rows + 16) * SUB, LANES)
        tail = ((rows + SUB) * SUB, LANES)
        V = pltpu.VMEM
        D = pltpu.SemaphoreType.DMA
        tile = (SUB, LANES)
        scratch = (
            [V((rows, cols), jnp.bfloat16)] * 4
            + [V((3, 16, cols), jnp.bfloat16)]
            + [V(front, F32)] * 3
            + [V(flat, F32)] * 8
            + [V((3, SUB * SUB, LANES), F32)]
            + [
                V(((reach + 1) * 3 * (reach + 1),) + tile, F32),
                V((2 * modes,) + tile, F32),
                V((5 * modes,) + tile, F32),
                V((SUB * SUB, LANES), F32),
                V((SUB * SUB, LANES), F32),
            ]
            + [V((rows + SUB, LANES), F32)] * 5
            + [
                V((2,) + tile, F32),
                V((2, n_tp) + tile, F32),
                V((2, n_ctx) + tile, F32),
                V((2, n_ctx) + tile, F32),
                V((2, n_ctx) + tile, F32),
                V((2, n_ctx) + tile, F32),
                V((3,) + tile, jnp.int32),
                pltpu.SMEM((3,) + tile, jnp.int32),
                V((3, reach + 1, cols), F32),
                V((modes, cols), F32),
                V((modes, cols), F32),
                V(tile, F32),
                V(tile, F32),
                pltpu.SMEM((2, docs), jnp.int32),
                D((4,)),
                D((6,)),
                D,
                D((3,)),
                D((3,)),
                D((2, 2, n_ctx)),
                D((2, 2, n_ctx)),
                D((2, n_tp)),
                D((2, n_tp)),
                D((3,)),
                D((3,)),
            ]
        )
        hbm = pl.BlockSpec(memory_space=pltpu.HBM)
        vmem = pl.BlockSpec(memory_space=pltpu.VMEM)
        out = jax.ShapeDtypeStruct((rows, cols), jnp.bfloat16)
        sizes = (n_ctx, n_tp, rows, docs, modes, reach)
        smem = pl.BlockSpec(memory_space=pltpu.SMEM)
        gain, spans = gain.reshape(SUB, LANES), spans.T
        held = [jax.ShapeDtypeStruct(tail, F32)] * 3
        held += [jax.ShapeDtypeStruct(flat, F32), jax.ShapeDtypeStruct((rows + SUB, LANES), F32)]
        args = (q, k, v, cot, taps, residue, decay, skip.reshape(SUB, LANES), gain, spans)
        args = [pltpu.with_memory_space_constraint(a, pltpu.HBM) for a in args]
        parts = pl.pallas_call(
            functools.partial(kernel, sizes),
            out_shape=held,
            in_specs=[hbm] * 10,
            out_specs=[vmem] * 5,
            scratch_shapes=scratch,
            compiler_params=pltpu.CompilerParams(
                collective_id=0, has_side_effects=True, vmem_limit_bytes=GRANT
            ),
            name="hyena",
        )(*args)
        return pl.pallas_call(
            functools.partial(finish, sizes),
            out_shape=(out,) * 4,
            in_specs=[vmem] * 5 + [hbm] * 3,
            out_specs=(hbm,) * 4,
            scratch_shapes=[
                V((3, reach + 1, cols), F32),
                V(tile, F32),
                pltpu.SMEM((2, docs), jnp.int32),
                D((3,)),
                V(flat, F32),
                V((4, rows, cols), jnp.bfloat16),
                V((SUB * SUB, LANES), F32),
                D((4, 2)),
            ],
            compiler_params=pltpu.CompilerParams(vmem_limit_bytes=LAST_GRANT),
            name="finish",
        )(*parts, args[4], args[8], args[9])

    placed = (
        P("ctx", "tp"),
        P("ctx", "tp"),
        P("ctx", "tp"),
        P(None, None, "tp"),
        P(None, "tp"),
        P(None, "tp"),
        P("tp"),
        P("tp"),
        P(),
        P("ctx", "tp"),
    )
    return jax.shard_map(
        local,
        mesh=mesh,
        in_specs=placed,
        out_specs=(P("ctx", "tp"),) * 4,
        check_vma=False,
    )
```
